32 devices in a mesh: gx: 2 (over y), gy: 4 (over z), gz: 4 (over x, core).
Axes of the slice: x: 2, y: 2, z: 4, core: 2. Of those that a mesh axis runs over, the one named last changes fastest.
Arguments:
- offsets: float32 [3, 8, 16, 16, 128], P(None, 'gx', 'gy', 'gz'), may hold values from 0 to 1
- burgers: float32 [3, 8, 16, 16, 128], P(None, 'gx', 'gy', 'gz'), may hold values from -6 to 6
- lines: float32 [3, 8, 16, 16, 128], P(None, 'gx', 'gy', 'gz'), may hold values from -3 to 3
- counts: int32 [8, 16, 16], P('gx', 'gy', 'gz'), may hold values from 1 to 128
- connect: int32 [2, 8, 16, 16, 128], P(None, 'gx', 'gy', 'gz'), may hold values from 0 to 8191
- node_pos: float32 [3, 2, 4, 4, 8192], P(None, 'gx', 'gy', 'gz'), may hold values from -6 to 6
- drag: float32 [2, 4, 4, 8192], P('gx', 'gy', 'gz'), may hold values from 0.5 to 4
- stress: float32 [3, 3], replicated, may hold values from -1 to 1
- shifts: int32 [2, 2, 4, 4], replicated, may hold values from 0 to 512, as said below
Outputs:
- migrated: float32 [6, 2, 4, 4, 9216], P(None, 'gx', 'gy', 'gz')
The draws below stay inside these ranges and needn't reach their ends.
Inputs may be any that keep to these rules, and one draw needn't show every extreme that they name: shifts[0] of the last domain along gx is 0 and shifts[1] of the first is 0; 512 is reached by both rows in every draw.
All inputs are finite; a program needn't handle non-finite values.
Results may differ from the reference program's by a relative error of at most 0.0003.
Values sent between devices are 32-bit elements; how exact they have to be, the bound alone decides.
A program may use at most 64 MiB of HBM per device.

```python
import math
import jax
import jax.numpy as jnp
from jax import lax

SEGS = 128
CX = 4
CY = 4
CZ = 4
NODES = 8192
MIG = 512
CAP = 9216
NX = 8
NY = 16
NZ = 16
N_GX = 2
N_GY = 4
N_GZ = 4


def draw_shifts(key, part):
    first_key, second_key = jax.random.split(jax.random.fold_in(key, 17))
    upward = jax.random.randint(first_key, (N_GX, N_GY, N_GZ), 0, MIG + 1)
    downward = jax.random.randint(second_key, (N_GX, N_GY, N_GZ), 0, MIG + 1)
    slab_index = lax.broadcasted_iota(jnp.int32, (N_GX, N_GY, N_GZ), 0)
    upward = jnp.where(slab_index == N_GX - 1, 0, upward)
    downward = jnp.where(slab_index == 0, 0, downward)
    upward = upward.at[0, 0, 0].set(MIG)
    downward = downward.at[N_GX - 1, 0, 0].set(MIG)
    return jnp.stack([upward, downward]).astype(jnp.int32)


def place_ends(array, rng, least, high):
    index_at = [jax.random.randint(jax.random.fold_in(rng, axis), (), 0, length) for axis, length in enumerate(array.shape)]
    longest = array.shape.index(max(array.shape))
    neighbour = index_at[:longest] + [(index_at[longest] + 1) % array.shape[longest]] + index_at[longest + 1:]
    return array.at[tuple(index_at)].set(least).at[tuple(neighbour)].set(high)


def shard_levels(own_key, dims, cuts, smallest, largest):
    gain = 1.0
    for axis_at, parts in cuts:
        heights = jax.random.uniform(jax.random.fold_in(jax.random.fold_in(own_key, 6), axis_at), (parts,), jnp.float32, smallest / len(cuts), largest / len(cuts))
        gain = gain * jnp.repeat(jnp.exp(heights), dims[axis_at] // parts).reshape((-1,) + (1,) * (len(dims) - 1 - axis_at))
    return gain


def noise(key, dims, width, reach, shards=(), kind=jnp.bfloat16):
    result = jax.random.normal(key, dims, jnp.float32) * width
    if len(shards) > 0:
        result = shard_levels(key, dims, shards, -0.22, 0.18) * result
    return jnp.clip(result, min=-reach, max=reach).astype(kind)


def setup_inputs(seed: int = 0) -> dict:
    arg_keys = jax.random.split(jax.random.key(seed), 10)
    offsets = jnp.clip(1.0 * jax.random.uniform(arg_keys[0], (3, NX, NY, NZ, SEGS), jnp.float32) ** shard_levels(arg_keys[0], (3, NX, NY, NZ, SEGS), ((1, 2), (2, 4), (3, 4)), -0.2, 0.2), 0.0, 1.0)
    burgers = noise(arg_keys[1], (3, NX, NY, NZ, SEGS), 1.0, 6.0, ((1, 2), (2, 4), (3, 4)), jnp.float32)
    lines = noise(arg_keys[2], (3, NX, NY, NZ, SEGS), 0.5, 3.0, ((1, 2), (2, 4), (3, 4)), jnp.float32)
    counts = place_ends(jax.random.randint(arg_keys[3], (NX, NY, NZ), 1, SEGS + 1), jax.random.fold_in(arg_keys[3], 1), 1, SEGS).astype(jnp.int32)
    connect = place_ends(jax.random.randint(arg_keys[4], (2, NX, NY, NZ, SEGS), 0, NODES), jax.random.fold_in(arg_keys[4], 1), 0, NODES - 1).astype(jnp.int32)
    node_pos = noise(arg_keys[5], (3, N_GX, N_GY, N_GZ, NODES), 1.0, 6.0, ((1, 2), (2, 4), (3, 4)), jnp.float32)
    drag = jnp.clip(jnp.exp(math.log(4.0) - 2.0794415 * jax.random.uniform(arg_keys[6], (N_GX, N_GY, N_GZ, NODES), jnp.float32) ** shard_levels(arg_keys[6], (N_GX, N_GY, N_GZ, NODES), ((0, 2), (1, 4), (2, 4)), -0.2, 0.2)), 0.5, 4.0)
    stress = jnp.clip(jax.random.uniform(arg_keys[7], (3, 3), jnp.float32, -1.0, 1.0), -1.0, 1.0)
    shifts = draw_shifts(jax.random.fold_in(arg_keys[9], 71), 0)
    return {"offsets": offsets, "burgers": burgers, "lines": lines, "counts": counts, "connect": connect, "node_pos": node_pos, "drag": drag, "stress": stress, "shifts": shifts}


SOFTEN_NEAR = 0.25
SOFTEN_FAR = 4.0
NEAR_SCALE = 0.0625
FAR_SCALE = 0.03125
TIME_STEP = 0.1
NEIGHBOURS = ((0, 0, 0), (1, 0, 0), (-1, 0, 0), (0, 1, 0), (0, -1, 0), (0, 0, 1), (0, 0, -1))

def as_index(value):
    return jnp.asarray(value).astype(jnp.int32)

def pair_term(target, source, offset):
    deltas = [target[axis_id][..., :, None] - source[axis_id][..., None, :] - float(offset[axis_id]) for axis_id in range(3)]
    radius = deltas[0] * deltas[0] + deltas[1] * deltas[1] + deltas[2] * deltas[2] + SOFTEN_NEAR
    inverse = lax.rsqrt(radius)
    burgers_dot = target[3][..., :, None] * source[3][..., None, :] + target[4][..., :, None] * source[4][..., None, :] + target[5][..., :, None] * source[5][..., None, :]
    line_dot = target[6][..., :, None] * source[6][..., None, :] + target[7][..., :, None] * source[7][..., None, :] + target[8][..., :, None] * source[8][..., None, :]
    weight = burgers_dot * line_dot * inverse * inverse * inverse
    return jnp.stack([lax.optimization_barrier(jnp.sum(weight * deltas[axis_id], axis=-1)) for axis_id in range(3)])

def far_stress(moments, centers, cells):
    distance = SOFTEN_FAR + jnp.zeros((cells.shape[1], centers.shape[1]), jnp.float32)
    for axis_id in range(3):
        gap = cells[axis_id][:, None] - centers[axis_id][None, :]
        distance = distance + gap * gap
    weights = lax.rsqrt(distance)
    return jnp.dot(moments, weights.T, precision=lax.Precision.HIGHEST, preferred_element_type=jnp.float32)

def segment_force(target, sigma):
    burgers = target[3:6]
    line = target[6:9]
    pulled = [sigma[row, 0][..., None] * burgers[0] + sigma[row, 1][..., None] * burgers[1] + sigma[row, 2][..., None] * burgers[2] for row in range(3)]
    return jnp.stack([pulled[1] * line[2] - pulled[2] * line[1], pulled[2] * line[0] - pulled[0] * line[2], pulled[0] * line[1] - pulled[1] * line[0]])

def coarse_moments(stacked):
    product = jnp.einsum('axyzk,bxyzk->abxyz', stacked[3:6], stacked[6:9], precision=lax.Precision.HIGHEST)
    sx, sy, sz = (product.shape[2], product.shape[3], product.shape[4])
    return product.reshape(9, sx // 2, 2, sy // 2, 2, sz // 2, 2).sum(axis=(2, 4, 6))

def migrate_index(up_prev, down_own, up_own, down_next, nodes, margin, capacity):
    position = lax.broadcasted_iota(jnp.int32, up_prev.shape + (capacity,), len(up_prev.shape))
    upper_in = up_prev[..., None]
    kept = (nodes - up_own - down_own)[..., None]
    source = jnp.where(position < upper_in, margin - upper_in + position, jnp.where(position < upper_in + kept, margin + down_own[..., None] + position - upper_in, margin + nodes + position - upper_in - kept))
    live = position < upper_in + kept + down_next[..., None]
    return (jnp.clip(source, 0, capacity - 1).astype(jnp.int32), live)

def reference(offsets, burgers, lines, counts, connect, node_pos, drag, stress, shifts):
    mask = (lax.broadcasted_iota(jnp.int32, (NX, NY, NZ, SEGS), 3) < counts[..., None]).astype(jnp.float32)
    stacked = jnp.concatenate([offsets, burgers * mask[None], lines], axis=0)
    padded = jnp.pad(stacked, ((0, 0), (1, 1), (1, 1), (1, 1), (0, 0)))
    moments = coarse_moments(stacked).reshape(9, -1)
    coarse_grid = (NX // 2, NY // 2, NZ // 2)
    centers = jnp.stack([(2 * lax.broadcasted_iota(jnp.int32, coarse_grid, axis_id) + 1).astype(jnp.float32).reshape(-1) for axis_id in range(3)])
    zero = as_index(0)

    def plane(index):
        index = as_index(index)
        target = lax.dynamic_slice(stacked, (zero, index, zero, zero, zero), (9, 1, NY, NZ, SEGS))
        near = jnp.zeros((3, 1, NY, NZ, SEGS), jnp.float32)
        for offset in NEIGHBOURS:
            starts = (zero, as_index(index + 1 + offset[0]), as_index(1 + offset[1]), as_index(1 + offset[2]), zero)
            source = lax.dynamic_slice(padded, starts, (9, 1, NY, NZ, SEGS))
            near = near + pair_term(target, source, offset)
        cell_x = jnp.zeros((NY, NZ), jnp.float32) + index.astype(jnp.float32) + 0.5
        cell_y = lax.broadcasted_iota(jnp.int32, (NY, NZ), 0).astype(jnp.float32) + 0.5
        cell_z = lax.broadcasted_iota(jnp.int32, (NY, NZ), 1).astype(jnp.float32) + 0.5
        cells = jnp.stack([cell_x.reshape(-1), cell_y.reshape(-1), cell_z.reshape(-1)])
        sigma = FAR_SCALE * far_stress(moments, centers, cells).reshape(3, 3, 1, NY, NZ) + stress[:, :, None, None, None]
        return NEAR_SCALE * near + segment_force(target, sigma)
    planes = lax.map(plane, jnp.arange(NX, dtype=jnp.int32))
    total = jnp.moveaxis(planes[:, :, 0], 0, 1)
    domain_x = lax.broadcasted_iota(jnp.int32, (NX, NY, NZ), 0) // CX
    domain_y = lax.broadcasted_iota(jnp.int32, (NX, NY, NZ), 1) // CY
    domain_z = lax.broadcasted_iota(jnp.int32, (NX, NY, NZ), 2) // CZ
    domain = (domain_x * N_GY + domain_y) * N_GZ + domain_z
    global_ids = (connect + (domain * NODES)[None, :, :, :, None]).astype(jnp.int32)
    halves = 0.5 * total.reshape(3, -1)
    values = jnp.concatenate([halves, halves], axis=1).T
    node_count = N_GX * N_GY * N_GZ * NODES
    node_force = jax.ops.segment_sum(values, global_ids.reshape(-1), num_segments=node_count).T
    node_force = node_force.reshape(3, N_GX, N_GY, N_GZ, NODES)
    velocity = node_force / drag[None]
    fields = jnp.concatenate([node_pos + TIME_STEP * velocity, velocity], axis=0)
    empty = jnp.zeros((6, 1, N_GY, N_GZ, MIG), jnp.float32)
    from_below = jnp.concatenate([empty, fields[:, :-1, :, :, NODES - MIG:]], axis=1)
    from_above = jnp.concatenate([fields[:, 1:, :, :, :MIG], empty], axis=1)
    sectioning = jnp.concatenate([from_below, fields, from_above], axis=4)
    zero_row = jnp.zeros((1, N_GY, N_GZ), jnp.int32)
    up_own = shifts[0]
    down_own = shifts[1]
    up_prev = jnp.concatenate([zero_row, up_own[:-1]], axis=0)
    down_next = jnp.concatenate([down_own[1:], zero_row], axis=0)
    source, live = migrate_index(up_prev, down_own, up_own, down_next, NODES, MIG, CAP)
    picked = jnp.take_along_axis(sectioning, jnp.broadcast_to(source[None], sectioning.shape), axis=4)
    return jnp.where(live[None], picked, 0.0)
```

```python
import functools

import jax
import jax.numpy as jnp
import numpy as np
from jax import lax
from jax.experimental import pallas as pl
from jax.experimental.pallas import tpu as pltpu
from jax.sharding import PartitionSpec as P

MIG = 512
SOFTEN_NEAR = 0.25
SOFTEN_FAR = 4.0
NEAR_SCALE = 0.0625
FAR_SCALE = 0.03125
TIME_STEP = 0.1
AXES = ("gx", "gy", "gz")
MESH = pl.DeviceIdType.MESH
VM = pl.BlockSpec(memory_space=pltpu.VMEM)
SM = pl.BlockSpec(memory_space=pltpu.SMEM)
LANES = 128
FEATURES = 64
SIDE = FEATURES // 2
F32, BF16 = jnp.float32, jnp.bfloat16


def rounded(value):
    return value.astype(BF16).astype(F32)


def split(value, pieces):
    parts = []
    for _ in range(pieces - 1):
        part = rounded(value)
        parts.append(part)
        value = value - part
    return parts + [value]


def source_features(place, bm, line, products):
    rows = {}
    norm = place[0] * place[0] + place[1] * place[1] + place[2] * place[2] + SOFTEN_NEAR
    for c in range(3):
        h, m, l = split(place[c], 3)
        for k, part in enumerate((h, m, l, h, m, h)):
            rows[6 * c + k] = part
    for k, part in enumerate(split(norm, 3)):
        rows[18 + k] = part
    one = jnp.ones_like(norm)
    for k in range(3):
        rows[21 + k] = one
    for n, product in enumerate(products):
        h, l = split(product, 2)
        for k, part in enumerate((h, l, h)):
            rows[SIDE + 3 * n + k] = part
    return rows


def target_features(place, products):
    rows = {}
    norm = place[0] * place[0] + place[1] * place[1] + place[2] * place[2]
    for c in range(3):
        h, m, l = split(-2.0 * place[c], 3)
        for k, part in enumerate((h, h, h, m, m, l)):
            rows[6 * c + k] = part
    one = jnp.ones_like(norm)
    for k in range(3):
        rows[18 + k] = one
    for k, part in enumerate(split(norm, 3)):
        rows[21 + k] = part
    for n, product in enumerate(products):
        h, l = split(product, 2)
        for k, part in enumerate((h, h, l)):
            rows[SIDE + 3 * n + k] = part
    return rows


def cycle_kernel(
    grid, sizes, counts, stress, off, bur, lin, origin, code, centers, groups, connect, pos, drag,
    fields, below, above, *scratch,
):
    (fx, fy, fz, hx, hy, hz, mom, gathered, bm, place, wide, weights, targets, spots, pair_a, pair_b,
     partial, raw, near, left, right, acc, low, high,
     face_send, face_recv, mom_send, mom_recv, own_sem, edge_send, edge_recv) = scratch
    cx, cy, cz = grid
    cells = cx * cy * cz
    nx, ny, nz = sizes
    index = [lax.axis_index(name) for name in AXES]
    barrier = pltpu.get_barrier_semaphore()
    peers = 0
    for name, me, n in zip(AXES, index, sizes):
        for d in range(1, n):
            pl.semaphore_signal(
                barrier, inc=1, device_id={name: lax.rem(me + d, n)}, device_id_type=MESH
            )
            peers += 1

    face = (cy * cz, cx * cz, cx * cy)
    base = [cells]
    for axis in range(3):
        base.append(base[-1] + 2 * face[axis])

    lane8 = lax.broadcasted_iota(jnp.int32, (8, LANES), 1)
    sub8 = lax.broadcasted_iota(jnp.int32, (8, LANES), 0)
    for block in range(cells // 8):
        live = jnp.zeros((8, LANES), jnp.int32)
        for k in range(8):
            t = block * 8 + k
            live = jnp.where(sub8 == k, counts[t // (cy * cz), t // cz % cy, t % cz], live)
        mask = lane8 < live
        for c in range(3):
            bm[c, block * 8 : block * 8 + 8, :] = jnp.where(
                mask, bur[c, block * 8 : block * 8 + 8, :], 0.0
            )
    for c in range(9):
        part = (off, bm, lin)[c // 3].at[c % 3]
        fx[0, c] = part[0 : cy * cz, :]
        fx[1, c] = part[cells - cy * cz : cells, :]
        for x in range(cx):
            start = x * cy * cz
            fy[0, c, x * cz : (x + 1) * cz, :] = part[start : start + cz, :]
            start = start + (cy - 1) * cz
            fy[1, c, x * cz : (x + 1) * cz, :] = part[start : start + cz, :]
        fz[0, c] = (off, bm, lin)[c // 3][c % 3, pl.ds(0, cx * cy, stride=cz), :]
        fz[1, c] = (off, bm, lin)[c // 3][c % 3, pl.ds(cz - 1, cx * cy, stride=cz), :]

    total = jnp.zeros((cells, LANES), F32)
    for a in range(3):
        for b in range(3):
            part = jnp.sum(bm[a] * lin[b], axis=1, keepdims=True)
            total = total + jnp.where(code[...] == 3 * a + b, part, 0.0)
    mom[0] = jnp.sum(total, axis=0, keepdims=True)

    empty = jnp.zeros((8, LANES), F32)

    def blank(t, carry):
        wide[pl.ds(pl.multiple_of(t * FEATURES + 24, 8), 8), :] = empty
        wide[pl.ds(pl.multiple_of(t * FEATURES + 56, 8), 8), :] = empty
        return carry

    lax.fori_loop(0, base[3], blank, 0)

    def blank_target(t, carry):
        targets[pl.ds(pl.multiple_of(t * FEATURES + 24, 8), 8), :] = empty
        targets[pl.ds(pl.multiple_of(t * FEATURES + 56, 8), 8), :] = empty
        return carry

    lax.fori_loop(0, cells, blank_target, 0)

    def put_source(start, count, where, bmv, linev):
        products = [bmv[a] * linev[b] for a in range(3) for b in range(3)]
        for k, value in source_features(where, bmv, linev, products).items():
            wide[pl.ds(start * FEATURES + k, count, stride=FEATURES), :] = value
        for c in range(3):
            spots[pl.ds(start * 8 + c, count, stride=8), :] = where[c]
        return products

    for start in range(0, cells, 16):
        span = slice(start, start + 16)
        where = [off[c, span, :] + origin[span, c : c + 1] for c in range(3)]
        for c in range(3):
            place[c, span, :] = where[c]
        bmv = [bm[c, span, :] for c in range(3)]
        linev = [lin[c, span, :] for c in range(3)]
        products = put_source(start, 16, where, bmv, linev)
        for k, value in target_features(where, products).items():
            targets[pl.ds(start * FEATURES + k, 16, stride=FEATURES), :] = value

    def narrow(t, carry):
        weights[t] = wide[pl.ds(pl.multiple_of(t * FEATURES, FEATURES), FEATURES), :].astype(BF16)
        return carry

    lax.fori_loop(0, cells, narrow, 0)

    pl.semaphore_wait(barrier, peers)

    def moment_copies(level, src, dst):
        name, me, n = AXES[level], index[level], sizes[level]
        first = sum(size - 1 for size in sizes[:level])
        return [
            pltpu.make_async_remote_copy(
                src_ref=src,
                dst_ref=dst,
                send_sem=mom_send.at[first + d - 1],
                recv_sem=mom_recv.at[first + d - 1],
                device_id={name: lax.rem(me + d, n)},
                device_id_type=MESH,
            )
            for d in range(1, n)
        ]

    row = (index[0] * ny + index[1]) * nz + index[2]
    own = pltpu.make_async_copy(mom, gathered.at[pl.ds(row, 1)], own_sem)
    own.start()
    row_block = gathered.at[pl.ds((index[0] * ny + index[1]) * nz, nz)]
    slab_block = gathered.at[pl.ds(index[0] * ny * nz, ny * nz)]
    levels = [
        moment_copies(2, mom, gathered.at[pl.ds(row, 1)]),
        moment_copies(1, row_block, row_block),
        moment_copies(0, slab_block, slab_block),
    ]
    for copy in levels[0]:
        copy.start()

    def face_copy(axis, src, halo, up):
        me, n = index[axis], sizes[axis]
        slot = 2 * axis + (0 if up else 1)
        return pltpu.make_async_remote_copy(
            src_ref=src.at[1 if up else 0],
            dst_ref=halo.at[0 if up else 1],
            send_sem=face_send.at[slot],
            recv_sem=face_recv.at[slot],
            device_id={AXES[axis]: lax.rem(me + 1, n) if up else lax.rem(me + n - 1, n)},
            device_id_type=MESH,
        )

    pairs = [(0, fx, hx), (1, fy, hy), (2, fz, hz)]
    for axis, src, halo in pairs:

        @pl.when(index[axis] < sizes[axis] - 1)
        def _():
            face_copy(axis, src, halo, True).start()

        @pl.when(index[axis] > 0)
        def _():
            face_copy(axis, src, halo, False).start()

    pitch = (cy * cz, cz, 1)

    def corner(t):
        x, rest = lax.div(t, cy * cz), lax.rem(t, cy * cz)
        y, z = lax.div(rest, cz), lax.rem(rest, cz)
        return (x, y, z), (y * cz + z, x * cz + z, x * cy + y)

    def inside_sources(t):
        spot, _ = corner(t)
        return [t] + [
            jnp.where(spot[axis] < grid[axis] - 1, t + pitch[axis], t - pitch[axis])
            for axis in range(3)
        ]

    def other_sources(t):
        spot, offset = corner(t)
        rows = []
        for axis in range(3):
            lower = jnp.where(spot[axis] > 0, t - pitch[axis], base[axis] + offset[axis])
            upper = base[axis] + face[axis] + offset[axis]
            rows.append(jnp.where(spot[axis] < grid[axis] - 1, lower, upper))
        return rows

    blank_half = jnp.zeros((SIDE, LANES), BF16)

    def products_of(t, sources, pair):
        tile = targets[pl.ds(pl.multiple_of(t * FEATURES, FEATURES), FEATURES), :]
        lhs = tile.T.astype(BF16)
        for k, source in enumerate(sources(t)):
            tile = weights[source]
            rhs = jnp.concatenate(
                [
                    jnp.concatenate([tile[0:SIDE], blank_half], axis=1),
                    jnp.concatenate([blank_half, tile[SIDE:FEATURES]], axis=1),
                ],
                axis=0,
            )
            pair[k] = jnp.dot(lhs, rhs, preferred_element_type=F32)

    def sums_of(t, sources, pair, first, last):
        rows = sources(t)
        spot = [
            [jnp.broadcast_to(spots[pl.ds(source * 8 + c, 1), :], (8, LANES)) for c in range(3)]
            for source in rows
        ]
        outs = []
        for h in range(LANES // 8):
            span = slice(8 * h, 8 * h + 8)
            sums = [None if first else partial[t, c, span, :] for c in range(4)]
            for k in range(len(rows)):
                inverse = lax.rsqrt(pair[k, span, 0:LANES])
                weight = pair[k, span, LANES : 2 * LANES] * (inverse * inverse * inverse)
                terms = [weight] + [weight * spot[k][c] for c in range(3)]
                sums = [term if old is None else old + term for old, term in zip(sums, terms)]
            if last:
                out = jnp.zeros((8, LANES), F32)
                for c in range(4):
                    out = jnp.where(lane8 == c, jnp.sum(sums[c], axis=1, keepdims=True), out)
                outs.append(out)
            else:
                for c in range(4):
                    partial[t, c, span, :] = sums[c]
        if last:
            full = jnp.concatenate(outs, axis=0)
            raw[pl.ds(pl.multiple_of(t * 8, 8), 8), :] = full.T[0:8]

    def sweep(sources, first, last):
        def body(i, carry):
            t = i * 2
            products_of(t + 1, sources, pair_b)
            sums_of(t, sources, pair_a, first, last)
            products_of(lax.rem(t + 2, cells), sources, pair_a)
            sums_of(t + 1, sources, pair_b, first, last)
            return carry

        return body

    steps = cells // 2
    products_of(0, inside_sources, pair_a)
    body = sweep(inside_sources, True, False)
    stages = 4

    def stage(s, carry):
        lax.fori_loop(s * (steps // stages), (s + 1) * (steps // stages), body, 0)
        for level in range(2):

            @pl.when(s == level)
            def _():
                if level == 0:
                    own.wait()
                for copy in levels[level]:
                    copy.wait_recv()
                for copy in levels[level + 1]:
                    copy.start()

        return carry

    lax.fori_loop(0, stages, stage, 0)

    for axis, src, halo in pairs:

        @pl.when(index[axis] > 0)
        def _():
            face_copy(axis, src, halo, True).wait_recv()

        @pl.when(index[axis] < sizes[axis] - 1)
        def _():
            face_copy(axis, src, halo, False).wait_recv()

    for axis, src, halo in pairs:
        for side in range(2):
            there = index[axis] < sizes[axis] - 1 if side else index[axis] > 0
            flag = jnp.full((face[axis], LANES), jnp.where(there, 1, 0), jnp.int32) > 0
            start = base[axis] + side * face[axis]
            value = [jnp.where(flag, halo[side, c], 0.0) for c in range(9)]
            span = slice(start, start + face[axis])
            where = [value[c] + origin[span, c : c + 1] for c in range(3)]
            put_source(start, face[axis], where, value[3:6], value[6:9])
    lax.fori_loop(cells, base[3], narrow, 0)

    products_of(0, other_sources, pair_a)
    lax.fori_loop(0, steps, sweep(other_sources, False, True), 0)

    for copy in levels[2]:
        copy.wait_recv()
    distance = jnp.full((cells, centers.shape[1]), SOFTEN_FAR, F32)
    for axis in range(3):
        middle = (index[axis] * grid[axis]).astype(F32) + (0.5 * grid[axis] + 0.5)
        gap = (origin[0:cells, axis : axis + 1] + middle) - centers[axis : axis + 1, :]
        distance = distance + gap * gap
    local = centers.shape[1] // gathered.shape[0]
    keep = lax.rem(lax.broadcasted_iota(jnp.int32, (local, LANES), 1), local) == (
        lax.broadcasted_iota(jnp.int32, (local, LANES), 0)
    )
    spread = jnp.concatenate(
        [
            jnp.where(keep, jnp.broadcast_to(gathered[d], (local, LANES)), 0.0)
            for d in range(gathered.shape[0])
        ],
        axis=0,
    )
    far = jnp.dot(
        lax.rsqrt(distance), spread, precision=lax.Precision.HIGHEST, preferred_element_type=F32
    )
    mixed = jnp.dot(
        far, groups[...], precision=lax.Precision.HIGHEST, preferred_element_type=F32
    )
    pulled = []
    for r in range(3):
        value = 0.0
        for c in range(3):
            sigma = FAR_SCALE * mixed[:, 3 * r + c : 3 * r + c + 1] + stress[r, c]
            value = value + sigma * bm[c]
        pulled.append(value)
    weight = raw[pl.ds(0, cells, stride=8), :]
    for c in range(3):
        a, b = (c + 1) % 3, (c + 2) % 3
        pull = place[c] * weight - raw[pl.ds(1 + c, cells, stride=8), :]
        force = NEAR_SCALE * pull + (pulled[a] * lin[b] - pulled[b] * lin[a])
        near[c] = 0.5 * force

    node_rows = pos.shape[1]
    half = node_rows // 2
    acc[...] = jnp.zeros_like(acc)
    slim = jnp.bfloat16
    high_ids = lax.broadcasted_iota(jnp.int32, (half, LANES), 0).astype(jnp.float32).astype(slim)
    low_ids = lax.broadcasted_iota(jnp.int32, (LANES, LANES), 0).astype(jnp.float32).astype(slim)
    groups_of = cells // 8
    zero = jnp.zeros((half, LANES), slim)

    def tall(row, count):
        piece = jnp.broadcast_to(row, (16, LANES)).astype(slim)
        return jnp.concatenate([piece] * (count // 16), axis=0)

    def scatter(step, carry):
        end, block = lax.div(step, groups_of), lax.rem(step, groups_of)
        start = pl.multiple_of(block * 8, 8)
        ids = connect[end, pl.ds(start, 8), :]
        values = [near[c, pl.ds(start, 8), :] for c in range(3)]
        parts = []
        for value in values:
            coarse = value.astype(slim).astype(jnp.float32)
            parts += [coarse, value - coarse]
        node_row = lax.shift_right_logical(ids, 7)
        upper = node_row >= half
        hi = jnp.where(upper, node_row - half, node_row).astype(jnp.float32)
        lo = (ids & (LANES - 1)).astype(jnp.float32)
        low_half = jnp.where(upper, -1.0, lo)
        high_half = jnp.where(upper, lo, -1.0)
        one, none = jnp.ones((LANES, LANES), slim), jnp.zeros((LANES, LANES), slim)
        for k in range(8):
            span = slice(k * LANES, (k + 1) * LANES)
            mask = high_ids == tall(hi[k : k + 1, :], half)
            for m, part in enumerate(parts):
                left[m * half : (m + 1) * half, span] = jnp.where(
                    mask, tall(part[k : k + 1, :], half), zero
                )
            right[0:LANES, span] = jnp.where(
                low_ids == tall(low_half[k : k + 1, :], LANES), one, none
            )
            right[LANES : 2 * LANES, span] = jnp.where(
                low_ids == tall(high_half[k : k + 1, :], LANES), one, none
            )
        acc[...] += lax.dot_general(
            left[...], right[...], (((1,), (1,)), ((), ())), preferred_element_type=jnp.float32
        )
        return carry

    lax.fori_loop(0, 2 * groups_of, scatter, 0)
    edge = low.shape[1]
    for c in range(3):
        both = acc[2 * c * half : (2 * c + 1) * half, :] + acc[(2 * c + 1) * half : (2 * c + 2) * half, :]
        for s in range(2):
            span = slice(s * half, (s + 1) * half)
            velocity = both[:, s * LANES : (s + 1) * LANES] / drag[span, :]
            fields[3 + c, span, :] = velocity
            fields[c, span, :] = pos[c, span, :] + TIME_STEP * velocity
    for c in range(6):
        low[c] = fields[c, 0:edge, :]
        high[c] = fields[c, node_rows - edge : node_rows, :]

    def edge_copy(slot, src, dst, peer):
        return pltpu.make_async_remote_copy(
            src_ref=src,
            dst_ref=dst,
            send_sem=edge_send.at[slot],
            recv_sem=edge_recv.at[slot],
            device_id={"gx": peer},
            device_id_type=MESH,
        )

    after, before = lax.rem(index[0] + 1, nx), lax.rem(index[0] + nx - 1, nx)
    upward = edge_copy(0, high, below, after)
    downward = edge_copy(1, low, above, before)

    @pl.when(index[0] < nx - 1)
    def _():
        upward.start()

    @pl.when(index[0] > 0)
    def _():
        downward.start()

    for axis, src, halo in pairs:

        @pl.when(index[axis] < sizes[axis] - 1)
        def _():
            face_copy(axis, src, halo, True).wait_send()

        @pl.when(index[axis] > 0)
        def _():
            face_copy(axis, src, halo, False).wait_send()

    for copy in levels[0] + levels[1] + levels[2]:
        copy.wait_send()

    @pl.when(index[0] < nx - 1)
    def _():
        upward.wait_send()
        downward.wait_recv()

    @pl.when(index[0] > 0)
    def _():
        downward.wait_send()
        upward.wait_recv()


def assemble_kernel(sizes, moves, fields, below, above, out, section):
    node_rows, edge, out_rows = fields.shape[1], below.shape[1], out.shape[1]
    nodes, margin = node_rows * LANES, edge * LANES
    section[:, 0:edge, :] = below[...]
    section[:, edge : edge + node_rows, :] = fields[...]
    section[:, edge + node_rows : 2 * edge + node_rows, :] = above[...]
    nx, ny, nz = sizes
    ix, iy, iz = [lax.axis_index(name) for name in AXES]
    at = lambda k, slab: moves[k, slab, iy, iz]
    up_own, down_own = at(0, ix), at(1, ix)
    up_prev = jnp.where(ix > 0, at(0, jnp.maximum(ix - 1, 0)), 0)
    down_next = jnp.where(ix < nx - 1, at(1, jnp.minimum(ix + 1, nx - 1)), 0)
    kept = nodes - up_own - down_own

    def shifted(c, by, first, count):
        row, turn = lax.div(by, LANES), lax.rem(by, LANES)
        lane = lax.broadcasted_iota(jnp.int32, (count, LANES), 1)
        back = lax.rem(LANES - turn, LANES)
        now = pltpu.roll(section[c, pl.ds(first + row, count), :], back, axis=1)
        later = pltpu.roll(section[c, pl.ds(first + row + 1, count), :], back, axis=1)
        return jnp.where(lane < LANES - turn, now, later)

    tail = out_rows - (4 * edge)
    position = (
        lax.broadcasted_iota(jnp.int32, (out_rows, LANES), 0) * LANES
        + lax.broadcasted_iota(jnp.int32, (out_rows, LANES), 1)
    )
    for c in range(6):
        out[c] = shifted(c, margin + down_own - up_prev, 0, out_rows)
        head = 2 * edge
        value = shifted(c, margin - up_prev, 0, head)
        out[c, 0:head, :] = jnp.where(position[0:head] < up_prev, value, out[c, 0:head, :])
        value = shifted(c, margin + nodes - up_prev - kept, tail, out_rows - tail)
        spot = position[tail:]
        value = jnp.where(spot < up_prev + kept, out[c, tail:out_rows, :], value)
        out[c, tail:out_rows, :] = jnp.where(spot < up_prev + kept + down_next, value, 0.0)


def shards(mesh, offsets, burgers, lines, counts, connect, node_pos, drag, stress, shifts):
    grid = offsets.shape[1:4]
    slots = offsets.shape[4]
    cells = grid[0] * grid[1] * grid[2]
    sizes = tuple(mesh.shape[name] for name in AXES)
    nx, ny, nz = sizes
    devices = nx * ny * nz
    half = [size // 2 for size in grid]
    local = half[0] * half[1] * half[2]
    nodes = node_pos.shape[4]
    node_rows, edge = nodes // LANES, MIG // LANES

    t = np.arange(cells)
    x, y, z = t // (grid[1] * grid[2]), t // grid[2] % grid[1], t % grid[2]
    coarse = ((x // 2) * half[1] + y // 2) * half[2] + z // 2
    lane = np.arange(LANES)
    code = np.where(lane[None, :] % local == coarse[:, None], lane[None, :] // local, -1)
    device = np.repeat(np.arange(devices), local)
    inner = np.tile(np.arange(local), devices)
    centers = np.stack(
        [
            2 * (device // (ny * nz) * half[0] + inner // (half[1] * half[2])) + 1,
            2 * (device // nz % ny * half[1] + inner // half[2] % half[1]) + 1,
            2 * (device % nz * half[2] + inner % half[2]) + 1,
        ]
    ).astype(np.float32)
    groups = (lane[:, None] // local == lane[None, :]).astype(np.float32)
    spots = [np.stack([x, y, z], axis=1)]
    for axis in range(3):
        plane = [np.arange(size) for size in grid]
        for at in (-1, grid[axis]):
            plane[axis] = np.array([at])
            spots.append(np.stack(np.meshgrid(*plane, indexing="ij"), axis=-1).reshape(-1, 3))
    spots = np.concatenate(spots)
    origin = np.zeros((spots.shape[0], LANES), np.float32)
    origin[:, 0:3] = spots - 0.5 * np.array(grid)

    flat = lambda array: array.reshape(array.shape[0], cells, slots)
    face = (grid[1] * grid[2], grid[0] * grid[2], grid[0] * grid[1])
    every = cells + 2 * sum(face)
    faces = [pltpu.VMEM((2, 9, size, slots), F32) for size in face]
    steps = sum(sizes) - 3
    dma = pltpu.SemaphoreType.DMA

    edge_shape = jax.ShapeDtypeStruct((6, edge, LANES), F32)
    fields, below, above = pl.pallas_call(
        functools.partial(cycle_kernel, grid, sizes),
        out_shape=[jax.ShapeDtypeStruct((6, node_rows, LANES), F32), edge_shape, edge_shape],
        in_specs=[SM] * 2 + [VM] * 10,
        out_specs=[VM] * 3,
        scratch_shapes=faces + faces
        + [
            pltpu.VMEM((1, 1, LANES), F32),
            pltpu.VMEM((devices, 1, LANES), F32),
            pltpu.VMEM((3, cells, LANES), F32),
            pltpu.VMEM((3, cells, LANES), F32),
            pltpu.VMEM((every * FEATURES, LANES), F32),
            pltpu.VMEM((every, FEATURES, LANES), BF16),
            pltpu.VMEM((cells * FEATURES, LANES), F32),
            pltpu.VMEM((every * 8, LANES), F32),
            pltpu.VMEM((4, LANES, 2 * LANES), F32),
            pltpu.VMEM((4, LANES, 2 * LANES), F32),
            pltpu.VMEM((cells, 4, LANES, LANES), F32),
            pltpu.VMEM((cells * 8, LANES), F32),
            pltpu.VMEM((3, cells, LANES), F32),
            pltpu.VMEM((3 * node_rows, 8 * LANES), BF16),
            pltpu.VMEM((2 * LANES, 8 * LANES), BF16),
            pltpu.VMEM((3 * node_rows, 2 * LANES), F32),
            pltpu.VMEM((6, edge, LANES), F32),
            pltpu.VMEM((6, edge, LANES), F32),
            dma((6,)), dma((6,)), dma((steps,)), dma((steps,)), dma, dma((2,)), dma((2,)),
        ],
        compiler_params=pltpu.CompilerParams(collective_id=0, has_side_effects=True),
        name="cycle",
    )(
        counts, stress,
        flat(offsets), flat(burgers), flat(lines),
        jnp.asarray(origin), jnp.asarray(code, jnp.int32), jnp.asarray(centers), jnp.asarray(groups),
        flat(connect), node_pos.reshape(3, node_rows, LANES), drag.reshape(node_rows, LANES),
    )

    out_rows = node_rows + 2 * edge
    result = pl.pallas_call(
        functools.partial(assemble_kernel, sizes),
        out_shape=jax.ShapeDtypeStruct((6, out_rows, LANES), F32),
        in_specs=[SM] + [VM] * 3,
        out_specs=VM,
        scratch_shapes=[pltpu.VMEM((6, out_rows + 4 * edge, LANES), F32)],
        name="assemble",
    )(shifts, fields, below, above)
    return result.reshape(6, 1, 1, 1, out_rows * LANES)


def solution(mesh):
    return jax.shard_map(
        functools.partial(shards, mesh),
        mesh=mesh,
        in_specs=(
            P(None, "gx", "gy", "gz", None),
            P(None, "gx", "gy", "gz", None),
            P(None, "gx", "gy", "gz", None),
            P("gx", "gy", "gz"),
            P(None, "gx", "gy", "gz", None),
            P(None, "gx", "gy", "gz", None),
            P("gx", "gy", "gz", None),
            P(),
            P(),
        ),
        out_specs=P(None, "gx", "gy", "gz", None),
        check_vma=False,
    )
```
